32 devices in a mesh: ctx: 8 (over z, y), ch: 4 (over x, core).
Axes of the slice: x: 2, y: 2, z: 4, core: 2. Of those that a mesh axis runs over, the one named last changes fastest.
Arguments:
- q_rows: bfloat16 [4096, 8192], P(('ctx', 'ch')), may hold values from -6 to 6
- k_rows: bfloat16 [4096, 8192], P(('ctx', 'ch')), may hold values from -6 to 6
- v_rows: bfloat16 [4096, 8192], P(('ctx', 'ch')), may hold values from -6 to 6
- short_taps: float32 [3, 3, 8192], replicated, may hold values from -3.5 to 3.5
- rates: float32 [512, 16], replicated, as said below
- freqs: float32 [512, 16], replicated, may hold values from 0 to 0.05
- residues: float32 [2, 512, 16], replicated, as said below
- skip: float32 [8192], replicated, may hold values from 0.5 to 1.5
Outputs:
- mixed: bfloat16 [4096, 8192], P(('ctx', 'ch'))
The draws below stay inside these ranges and needn't reach their ends.
Inputs may be any that keep to these rules, and one draw needn't show every extreme that they name: Positive decay rates. Real and imaginary residues of order a few tenths.
All inputs are finite; a program needn't handle non-finite values.
Results may differ from the reference program's by a relative error of at most 0.0058.
Values may be sent and summed in bfloat16 or wider, within the bound.
A program may use at most 192 MiB of HBM per device.

```python
import math
import jax
import jax.numpy as jnp
from jax import lax

D = 8192
GROUP_WIDTH = 16
MODES = 16
GROUPS = 512
SEQ = 4096


def modal_rates(key):
    pick_key, slow_key, fast_key = jax.random.split(jax.random.fold_in(key, 101), 3)
    share = 0.5
    slow_pick = jax.random.bernoulli(pick_key, share, (GROUPS, MODES))
    slow = jnp.exp(jax.random.uniform(slow_key, (GROUPS, MODES), jnp.float32, math.log(0.1 / SEQ), math.log(2.0 / SEQ)))
    fast = jnp.exp(jax.random.uniform(fast_key, (GROUPS, MODES), jnp.float32, math.log(2.0 / SEQ), math.log(0.05)))
    return jnp.where(slow_pick, slow, fast)


def draw_rates(key, part):
    return modal_rates(key)


def draw_residues(key, part):
    rates = modal_rates(key)
    noise_key = jax.random.fold_in(key, 202)
    base = jax.random.normal(noise_key, (2, GROUPS, MODES), jnp.float32)
    return base * 0.35 * jnp.sqrt(2.0 * rates + 4.0 / SEQ)[None]


def steps_of(key, dims, cuts, least, high):
    factor_of, own = 1.0, jax.random.fold_in(key, 6)
    for position, parts in cuts:
        steps = jnp.exp(jax.random.uniform(jax.random.fold_in(own, position), (parts,), jnp.float32, least / len(cuts), high / len(cuts)))
        factor_of = factor_of * jnp.repeat(steps, dims[position] // parts).reshape([-1 if axis == position else 1 for axis in range(len(dims))])
    return factor_of


def scatter_about(own_key, dims, spread, limit, cuts=(), held_as=jnp.bfloat16):
    drawn = jax.random.normal(own_key, dims, jnp.float32) * spread
    if len(cuts) > 0:
        drawn = steps_of(own_key, dims, cuts, -0.22, 0.18) * drawn
    return jnp.clip(drawn, min=-limit, max=limit).astype(held_as)


def setup_inputs(seed: int = 0) -> dict:
    keys = jax.random.split(jax.random.key(seed), 9)
    q_rows = scatter_about(keys[0], (SEQ, D), 1.0, 6.0, ((0, 32),))
    k_rows = scatter_about(keys[1], (SEQ, D), 1.0, 6.0, ((0, 32),))
    v_rows = scatter_about(keys[2], (SEQ, D), 1.0, 6.0, ((0, 32),))
    short_taps = scatter_about(keys[3], (3, 3, D), 3 ** -0.5, 3.5, (), jnp.float32)
    rates = draw_rates(jax.random.fold_in(keys[8], 71), 0)
    freqs = jnp.clip(jax.random.uniform(keys[5], (GROUPS, MODES), jnp.float32, 0.0, 0.05), 0.0, 0.05)
    residues = draw_residues(jax.random.fold_in(keys[8], 71), 0)
    skip = jnp.clip(jax.random.uniform(keys[7], (D,), jnp.float32, 0.5, 1.5), 0.5, 1.5)
    return dict(q_rows=q_rows, k_rows=k_rows, v_rows=v_rows, short_taps=short_taps, rates=rates, freqs=freqs, residues=residues, skip=skip)


def featurize(rows, taps):
    values = rows.astype(jnp.float32)
    zero_rows = jnp.zeros((2, values.shape[1]), jnp.float32)
    padded = jnp.concatenate([zero_rows, values], axis=0)
    return taps[0] * padded[2:] + taps[1] * padded[1:-1] + taps[2] * padded[:-2]


def filter_taps(rates, freqs, residues, length):
    times = jnp.arange(length).astype(jnp.float32)
    total = jnp.zeros((rates.shape[0], length), jnp.float32)
    for mode in range(rates.shape[1]):
        decay = jnp.exp(-rates[:, mode:mode + 1] * times[None])
        angle = freqs[:, mode:mode + 1] * times[None]
        total = total + decay * (residues[0][:, mode:mode + 1] * jnp.cos(angle) - residues[1][:, mode:mode + 1] * jnp.sin(angle))
    return total


def reference(q_rows, k_rows, v_rows, short_taps, rates, freqs, residues, skip):
    width = math.gcd(D, 256)
    count = D // width
    per_group = width // GROUP_WIDTH

    def column_block(index):
        start = index * width
        q_part = lax.dynamic_slice_in_dim(q_rows, start, width, 1)
        k_part = lax.dynamic_slice_in_dim(k_rows, start, width, 1)
        v_part = lax.dynamic_slice_in_dim(v_rows, start, width, 1)
        taps = lax.dynamic_slice_in_dim(short_taps, start, width, 2)
        q_feat = featurize(q_part, taps[0])
        k_feat = featurize(k_part, taps[1])
        v_feat = featurize(v_part, taps[2])
        gated = (k_feat * v_feat).astype(jnp.bfloat16)
        first = index * per_group
        kernel = filter_taps(lax.dynamic_slice_in_dim(rates, first, per_group, 0),
                             lax.dynamic_slice_in_dim(freqs, first, per_group, 0),
                             lax.dynamic_slice_in_dim(residues, first, per_group, 1), SEQ)
        kernel = jnp.repeat(kernel, GROUP_WIDTH, axis=0).T
        signal = lax.optimization_barrier(gated).astype(jnp.float32)
        size = 2 * SEQ
        spectrum = jnp.fft.rfft(signal, n=size, axis=0) * jnp.fft.rfft(kernel, n=size, axis=0)
        conv = jnp.fft.irfft(spectrum, n=size, axis=0)[:SEQ]
        gain = lax.dynamic_slice_in_dim(skip, start, width, 0)
        conv = (conv + gain[None] * signal).astype(jnp.bfloat16)
        conv = lax.optimization_barrier(conv).astype(jnp.float32)
        return (q_feat * conv).astype(jnp.bfloat16)

    pieces = lax.map(column_block, jnp.arange(count, dtype=jnp.int32))
    return jnp.transpose(pieces, (1, 0, 2)).reshape(SEQ, D)
```

```python
import jax
import jax.numpy as jnp
from jax import lax
from jax.experimental import pallas as pl
from jax.experimental.pallas import tpu as pltpu
from jax.sharding import PartitionSpec as P

GROUP_WIDTH = 16
MODES = 16
HALF = 128
LANES = 128
PACK = LANES // GROUP_WIDTH
STATE = 2 * MODES


def complex_power(decay, angle, steps):
    amplitude = jnp.exp(-decay * steps)
    return amplitude * jnp.cos(angle * steps), amplitude * jnp.sin(angle * steps)


def mode_table(decay, angle, coef, coarse, fine):
    hr, hi = complex_power(decay[None], angle[None], coarse[:, None])
    hr, hi = coef[0] * hr - coef[1] * hi, coef[0] * hi + coef[1] * hr
    lr, li = complex_power(decay[None], angle[None], fine[:, None])
    full = hr[:, None] * lr[None] - hi[:, None] * li[None]
    return full.reshape(coarse.shape[0] * fine.shape[0], -1).astype(jnp.bfloat16)


def shifted(rows, prior, by):
    moved = pltpu.roll(rows, by, 0)
    index = lax.broadcasted_iota(jnp.int32, rows.shape, 0)
    for row in range(by):
        moved = jnp.where(index == row, prior[2 - by + row : 3 - by + row], moved)
    return moved


def featurize(rows_ref, prior, taps):
    rows = rows_ref[...].astype(jnp.float32)
    return (
        taps[0:1] * rows
        + taps[1:2] * shifted(rows, prior, 1)
        + taps[2:3] * shifted(rows, prior, 2)
    )


def gate_kernel(k_ref, v_ref, prior_ref, taps_ref, out_ref):
    prior = prior_ref[...].astype(jnp.float32)
    k_feat = featurize(k_ref, prior[2:4], taps_ref[1])
    v_feat = featurize(v_ref, prior[4:6], taps_ref[2])
    out_ref[0] = (k_feat * v_feat).astype(jnp.bfloat16)


def mix_kernel(q_ref, prior_ref, taps_ref, conv_ref, out_ref):
    prior = prior_ref[...].astype(jnp.float32)
    q_feat = featurize(q_ref, prior[0:2], taps_ref[0])
    out_ref[...] = (q_feat * conv_ref[0].astype(jnp.float32)).astype(jnp.bfloat16)


def advance(power, state):
    pr, pi = power[:MODES], power[MODES:]
    sr, si = state[:MODES], state[MODES:]
    return jnp.concatenate([pr * sr - pi * si, pr * si + pi * sr], axis=0)


def own_group(rows):
    shape = (PACK * rows, LANES)
    row = lax.broadcasted_iota(jnp.int32, shape, 0) // rows
    lane = lax.broadcasted_iota(jnp.int32, shape, 1) // GROUP_WIDTH
    return row == lane


def summary_kernel(x_ref, reader_ref, power_ref, earlier_ref, own_ref):
    blocks = x_ref.shape[0] // HALF
    mask = own_group(STATE)
    reader = reader_ref[...]
    power = power_ref[...]
    state = jnp.zeros((STATE, LANES), jnp.float32)
    for block in range(blocks):
        rows = x_ref[block * HALF : (block + 1) * HALF, :]
        full = lax.dot_general(
            reader, rows, (((0,), (0,)), ((), ())), preferred_element_type=jnp.float32
        )
        entry = jnp.where(mask, full, 0.0).reshape(PACK, STATE, LANES).sum(axis=0)
        earlier_ref[block * STATE : (block + 1) * STATE, :] = state
        state = advance(power, state) + entry
    own_ref[0] = state


def conv_kernel(
    x_ref, taps_ref, writer_ref, earlier_ref, carry_ref, power_ref, gain_ref, out_ref, left, right
):
    blocks = x_ref.shape[0] // HALF
    row = lax.broadcasted_iota(jnp.int32, (HALF, HALF), 0)
    lane = lax.broadcasted_iota(jnp.int32, (HALF, HALF), 1)
    causal = lane <= row
    for group in range(PACK):
        wide = jnp.broadcast_to(taps_ref[group : group + 1, :], (HALF, HALF))
        turned = pltpu.roll(wide, 0, 1, stride=1, stride_axis=0)
        left[:, group * HALF : (group + 1) * HALF] = jnp.where(causal, turned, 0.0).astype(
            jnp.bfloat16
        )
    left[:, PACK * HALF :] = writer_ref[...]
    mask = own_group(STATE)
    lane_group = lane // GROUP_WIDTH
    power = power_ref[...]
    gain = gain_ref[...]
    lifted = carry_ref[0]
    for block in range(blocks):
        cols = slice(block * LANES, (block + 1) * LANES)
        rows = x_ref[block * HALF : (block + 1) * HALF, :].astype(jnp.float32)
        for group in range(PACK):
            right[group * HALF : (group + 1) * HALF, cols] = jnp.where(
                lane_group == group, rows, 0.0
            ).astype(jnp.bfloat16)
        state = earlier_ref[block * STATE : (block + 1) * STATE, :] + lifted
        spread = jnp.where(mask, jnp.concatenate([state] * PACK, axis=0), 0.0)
        right[PACK * HALF :, cols] = spread.astype(jnp.bfloat16)
        lifted = advance(power, lifted)
    step = 2 if blocks % 2 == 0 else 1
    for first in range(0, blocks, step):
        total = jnp.dot(
            left[...],
            right[:, first * LANES : (first + step) * LANES],
            preferred_element_type=jnp.float32,
        )
        for inner in range(step):
            span = slice((first + inner) * HALF, (first + inner + 1) * HALF)
            part = total[:, inner * LANES : (inner + 1) * LANES]
            out_ref[span, :] = (part + gain * x_ref[span, :].astype(jnp.float32)).astype(
                jnp.bfloat16
            )


def body(q_rows, k_rows, v_rows, short_taps, rates, freqs, residues, skip):
    members = lax.axis_size("ch")
    tracts = lax.axis_size("ctx")
    size = members * tracts
    count, width = q_rows.shape
    share = width // members
    share_groups = share // GROUP_WIDTH
    length = count * members
    blocks = length // HALF
    lane_blocks = share // LANES
    me = lax.axis_index("ch")

    tails = jnp.concatenate([q_rows[-2:], k_rows[-2:], v_rows[-2:]], axis=0)
    prior = lax.ppermute(tails, ("ctx", "ch"), [(i, i + 1) for i in range(size - 1)])

    tile = 1024
    per = share // tile
    rows_spec = pl.BlockSpec((count, tile), lambda j: (0, j))
    prior_spec = pl.BlockSpec((6, tile), lambda j: (0, j))
    taps_spec = pl.BlockSpec((3, 3, tile), lambda j: (0, 0, j))
    split_spec = pl.BlockSpec((1, count, tile), lambda j: (j // per, 0, j % per))
    gated = pl.pallas_call(
        gate_kernel,
        grid=(width // tile,),
        in_specs=[rows_spec, rows_spec, prior_spec, taps_spec],
        out_specs=split_spec,
        out_shape=jax.ShapeDtypeStruct((members, count, share), jnp.bfloat16),
        cost_estimate=pl.CostEstimate(
            flops=12 * count * width, bytes_accessed=6 * count * width, transcendentals=0
        ),
    )(k_rows, v_rows, prior, short_taps)
    signal = lax.all_to_all(gated, "ch", split_axis=0, concat_axis=0).reshape(length, share)

    first = me * share_groups
    decay = lax.dynamic_slice_in_dim(rates, first, share_groups, 0)
    angle = lax.dynamic_slice_in_dim(freqs, first, share_groups, 0)
    res = lax.dynamic_slice_in_dim(residues, first, share_groups, 1)
    gain = lax.dynamic_slice_in_dim(skip, me * share, share, 0)[None]
    decay2 = jnp.concatenate([decay, decay], axis=1).reshape(-1)
    angle2 = jnp.concatenate([angle, angle], axis=1).reshape(-1)
    ones, zeros = jnp.ones_like(decay), jnp.zeros_like(decay)
    read_coef = (
        jnp.concatenate([ones, zeros], axis=1).reshape(-1),
        jnp.concatenate([zeros, -ones], axis=1).reshape(-1),
    )
    write_coef = (
        jnp.concatenate([res[0], -res[1]], axis=1).reshape(-1),
        jnp.concatenate([res[1], res[0]], axis=1).reshape(-1),
    )
    coarse = jnp.arange(HALF // 16).astype(jnp.float32) * 16.0
    fine = jnp.arange(16).astype(jnp.float32)
    reader = mode_table(decay2, angle2, read_coef, coarse[::-1], fine[::-1])
    writer = mode_table(decay2, angle2, write_coef, coarse + 1.0, fine)
    back = lax.rem(HALF - jnp.arange(HALF), HALF).astype(jnp.float32)[None, None]
    tap_re, tap_im = complex_power(decay[:, :, None], angle[:, :, None], back)
    taps = jnp.sum(res[0][:, :, None] * tap_re - res[1][:, :, None] * tap_im, axis=1)
    chan_decay = jnp.repeat(decay.T, GROUP_WIDTH, axis=1)
    chan_angle = jnp.repeat(angle.T, GROUP_WIDTH, axis=1)
    power = jnp.concatenate(complex_power(chan_decay, chan_angle, float(HALF)), axis=0)

    piece = share // tracts
    sub = piece // LANES
    signal_spec = pl.BlockSpec((length, LANES), lambda j: (0, j))
    table_spec = pl.BlockSpec((HALF, PACK * STATE), lambda j: (0, j))
    state_spec = pl.BlockSpec((STATE, LANES), lambda j: (0, j))
    earlier_spec = pl.BlockSpec((blocks * STATE, LANES), lambda j: (0, j))
    relay_spec = pl.BlockSpec((1, STATE, LANES), lambda j: (j // sub, 0, j % sub))
    earlier, own = pl.pallas_call(
        summary_kernel,
        grid=(lane_blocks,),
        in_specs=[signal_spec, table_spec, state_spec],
        out_specs=[earlier_spec, relay_spec],
        out_shape=[
            jax.ShapeDtypeStruct((blocks * STATE, share), jnp.float32),
            jax.ShapeDtypeStruct((tracts, STATE, piece), jnp.float32),
        ],
    )(signal, reader, power)

    gathered = lax.all_to_all(own, "ctx", split_axis=0, concat_axis=0)
    mine = lax.axis_index("ctx") * piece
    tract_power = complex_power(
        lax.dynamic_slice_in_dim(chan_decay, mine, piece, 1),
        lax.dynamic_slice_in_dim(chan_angle, mine, piece, 1),
        float(length),
    )
    tract_power = jnp.concatenate(tract_power, axis=0)
    state = jnp.zeros((STATE, piece), jnp.float32)
    incoming = []
    for tract in range(tracts):
        incoming.append(state)
        state = advance(tract_power, state) + gathered[tract]
    carry = lax.all_to_all(jnp.stack(incoming), "ctx", split_axis=0, concat_axis=0)

    conv = pl.pallas_call(
        conv_kernel,
        grid=(lane_blocks,),
        in_specs=[
            signal_spec,
            pl.BlockSpec((PACK, HALF), lambda j: (j, 0)),
            table_spec,
            earlier_spec,
            relay_spec,
            state_spec,
            pl.BlockSpec((1, LANES), lambda j: (0, j)),
        ],
        out_specs=signal_spec,
        out_shape=jax.ShapeDtypeStruct((length, share), jnp.bfloat16),
        scratch_shapes=[
            pltpu.VMEM((HALF, PACK * (HALF + STATE)), jnp.bfloat16),
            pltpu.VMEM((PACK * (HALF + STATE), blocks * LANES), jnp.bfloat16),
        ],
    )(signal, taps, writer, earlier, carry, power, gain)

    conv_rows = lax.all_to_all(
        conv.reshape(members, count, share), "ch", split_axis=0, concat_axis=0
    )
    return pl.pallas_call(
        mix_kernel,
        grid=(width // tile,),
        in_specs=[rows_spec, prior_spec, taps_spec, split_spec],
        out_specs=rows_spec,
        out_shape=jax.ShapeDtypeStruct((count, width), jnp.bfloat16),
    )(q_rows, prior, short_taps, conv_rows)


def solution(mesh):
    rows = P(("ctx", "ch"), None)
    return jax.shard_map(
        body,
        mesh=mesh,
        in_specs=(rows, rows, rows, P(), P(), P(), P(), P()),
        out_specs=rows,
        check_vma=False,
    )
```
